32 devices in a mesh: feat: 8 (over z, y), layer: 4 (over x, core).
Axes of the slice: x: 2, y: 2, z: 4, core: 2. Of those that a mesh axis runs over, the one named last changes fastest.
Arguments:
- resid_in: bfloat16 [4, 512, 2304], P('layer', 'feat'), may hold values from -6 to 6
- enc_weight: bfloat16 [4, 2304, 4096], P('layer', None, 'feat'), may hold values from -0.125 to 0.125
- enc_bias: float32 [4, 4096], P('layer', 'feat'), may hold values from -3 to 3
- dec_weight: bfloat16 [4, 4, 4096, 2304], P('layer', None, 'feat'), may hold values from -0.09375 to 0.09375
- dec_bias: float32 [4, 2304], P('layer'), may hold values from -3 to 3
Outputs:
- recon: bfloat16 [4, 512, 2304], P('layer', 'feat')
The draws below stay inside these ranges and needn't reach their ends.
All inputs are finite; a program needn't handle non-finite values.
Results may differ from the reference program's by a relative error of at most 0.0046.
Values may be sent and summed in bfloat16 or wider, within the bound.
No kernel may reach another device: no remote copies, remote signals or barrier semaphores. Data moves between devices by JAX's collectives and lax.ppermute only.
A program may use at most 128 MiB of HBM per device.

```python
import jax
import jax.numpy as jnp

D = 2304
TOKENS = 512
F = 4096
LAYERS = 4


def level_of(stream_key, shape, pieces, smallest, top_value):
    factor_of = 1.0
    for axis_at, parts in pieces:
        heights = jax.random.uniform(jax.random.fold_in(jax.random.fold_in(stream_key, 6), axis_at), (parts,), jnp.float32, smallest / len(pieces), top_value / len(pieces))
        factor_of = factor_of * jnp.repeat(jnp.exp(heights), shape[axis_at] // parts).reshape((-1,) + (1,) * (len(shape) - 1 - axis_at))
    return factor_of


def bell_draw(rng, dims, scale, reach, split=(), held_as=jnp.bfloat16):
    entries = scale * jax.random.normal(rng, dims, jnp.float32)
    if split:
        entries = entries * level_of(rng, dims, split, -0.22, 0.18)
    return jnp.clip(entries, -reach, reach).astype(held_as)


def setup_inputs(seed: int = 0) -> dict:
    splits = jax.random.split(jax.random.key(seed), 6)
    return {
        "resid_in": bell_draw(splits[0], (LAYERS, TOKENS, D), 1.0, 6.0, ((0, 4), (1, 8))),
        "enc_weight": bell_draw(splits[1], (LAYERS, D, F), D ** -0.5, 0.125, ((0, 4), (2, 8))),
        "enc_bias": bell_draw(splits[2], (LAYERS, F), 0.5, 3.0, ((0, 4), (1, 8)), jnp.float32),
        "dec_weight": bell_draw(splits[3], (LAYERS, LAYERS, F, D), F ** -0.5, 0.09375, ((0, 4), (2, 8))),
        "dec_bias": bell_draw(splits[4], (LAYERS, D), 0.5, 3.0, ((0, 4),), jnp.float32),
    }


def reference(resid_in, enc_weight, enc_bias, dec_weight, dec_bias):
    actives = []
    for layer_idx in range(LAYERS):
        preact = jnp.dot(resid_in[layer_idx], enc_weight[layer_idx], preferred_element_type=jnp.float32) + enc_bias[layer_idx][None, :]
        actives.append(jnp.maximum(preact, 0.0).astype(jnp.bfloat16))
    outputs = []
    for target in range(LAYERS):
        summed = jnp.zeros((TOKENS, D), jnp.float32)
        for source in range(target + 1):
            summed = summed + jnp.dot(actives[source], dec_weight[source, target], preferred_element_type=jnp.float32)
        outputs.append((summed + dec_bias[target][None, :]).astype(jnp.bfloat16))
    return jnp.stack(outputs, axis=0)
```

```python
import jax
import jax.numpy as jnp
from jax import lax
from jax.sharding import PartitionSpec as P

CROSS = 2
SPLIT_AG = True


def gathered_form(resid_in, enc_weight, enc_bias, dec_weight, dec_bias):
    preact = (
        jnp.dot(
            lax.all_gather(resid_in, "feat", axis=1, tiled=True)[0],
            enc_weight[0],
            preferred_element_type=jnp.float32,
        )
        + enc_bias[0][None, :]
    )
    actives = jnp.maximum(preact, 0.0).astype(jnp.bfloat16)[None]
    source = lax.axis_index("layer")
    total_rows = actives.shape[1]
    model_width = dec_weight.shape[3]
    incoming = lax.all_to_all(dec_weight, "layer", split_axis=1, concat_axis=0, tiled=True)
    every_actives = lax.all_gather(actives, "layer", axis=0, tiled=True)

    def accumulate(earlier, running):
        weight = lax.dynamic_index_in_dim(incoming, earlier, 0, keepdims=False)[0]
        rows = lax.dynamic_index_in_dim(every_actives, earlier, 0, keepdims=False)
        return running + jnp.dot(rows, weight, preferred_element_type=jnp.float32)

    start_sum = jnp.zeros((total_rows, model_width), jnp.float32)
    own_sum = lax.fori_loop(0, source + 1, accumulate, start_sum)
    summed = lax.psum_scatter(own_sum[None], "feat", scatter_dimension=1, tiled=True)
    return (summed + dec_bias[:, None, :]).astype(jnp.bfloat16)


def ring_of(size):
    return list(range(0, size, 2)) + list(range(size - 1, 0, -2))


def ring_form(size, resid_in, enc_weight, enc_bias, dec_weight, dec_bias):
    far = size // 2
    order = ring_of(size)
    ahead = [(order[i], order[(i + 1) % size]) for i in range(size)]
    back = [(b, a) for a, b in ahead]
    swap = [(0, 1), (1, 0), (2, 3), (3, 2)]
    over = [(0, 2), (1, 3)]

    def step(value, pairs):
        return lax.ppermute(value, "feat", pairs)

    layer = lax.axis_index("layer")
    core = layer % 2
    rows = resid_in[0]
    half = rows.shape[0] // 2

    def decoder(target):
        return lax.dynamic_index_in_dim(dec_weight[0], target, 0, keepdims=False)

    near_other = lax.ppermute(decoder(jnp.minimum(layer + 1, 3)), "layer", [(0, 1), (2, 3)])
    upper_other = lax.ppermute(decoder(3 - core), "layer", [(0, 1), (1, 0)])
    near = jnp.concatenate([decoder(layer), near_other], axis=0)
    upper = jnp.concatenate([decoder(2 + core), upper_other], axis=0)

    if SPLIT_AG:
        a, b = rows[:half], rows[half:]
        fwd = [(a, b)]
        bwd = [(a, b)]
        for _ in range(1, far):
            fwd.append(tuple(step(v, ahead) for v in fwd[-1]))
            bwd.append(tuple(step(v, back) for v in bwd[-1]))
        last = jnp.concatenate([step(fwd[-1][0], ahead), step(bwd[-1][1], back)], axis=0)
        chunks = [rows] + [jnp.concatenate(fwd[d] + bwd[d], axis=0) for d in range(1, far)] + [last]
    else:
        fwd = [rows]
        bwd = [rows]
        for _ in range(1, far):
            fwd.append(step(fwd[-1], ahead))
            bwd.append(step(bwd[-1], back))
        last = jnp.concatenate([step(fwd[-1][:half], ahead), step(bwd[-1][half:], back)], axis=0)
        chunks = [rows] + [jnp.concatenate([fwd[d], bwd[d]], axis=0) for d in range(1, far)] + [last]

    def partials(chunk):
        preact = jnp.dot(chunk, enc_weight[0], preferred_element_type=jnp.float32) + enc_bias[0][None, :]
        own = jnp.maximum(preact, 0.0).astype(jnp.bfloat16)
        other = lax.ppermute(own, "layer", swap)
        both = jnp.concatenate([own, other], axis=1)
        return [
            jnp.dot(both, w, preferred_element_type=jnp.float32).astype(jnp.bfloat16)
            for w in (near, upper)
        ]

    count = rows.shape[0]
    made = [partials(c) for c in chunks]

    def piece(which, distance, forward):
        full = made[distance][which]
        if distance == 0:
            return full
        if distance == far:
            return full[:half] if forward else full[half:]
        return full[count:] if forward else full[:count]

    def plus(*values):
        total = values[0].astype(jnp.float32)
        for v in values[1:]:
            total = total + v.astype(jnp.float32)
        return total.astype(jnp.bfloat16)

    def widen(value, base, forward):
        if forward:
            return jnp.concatenate([plus(value, base[:half]), base[half:]], axis=0)
        return jnp.concatenate([base[:half], plus(value, base[half:])], axis=0)

    crossed = {}

    def cross(value):
        return lax.ppermute(value, "layer", over)

    for distance in range(0, CROSS):
        if distance == 0:
            crossed[0] = [cross(piece(1, 0, True))]
        else:
            for forward in (True, False):
                crossed[distance, forward] = cross(piece(1, distance, forward))

    def chain(which, forward, stop):
        pairs = ahead if forward else back
        value = piece(which, far, forward)
        for distance in range(far - 1, stop - 1, -1):
            got = step(value, pairs)
            if distance == 0:
                return got
            base = piece(which, distance, forward)
            extra = [crossed[distance, forward]] if which == 0 and (distance, forward) in crossed else []
            if distance == far - 1:
                value = widen(got, plus(base, *extra) if extra else base, forward)
            else:
                value = plus(got, base, *extra)
        return value

    if CROSS == 0:
        ends = [chain(1, f, 0) for f in (True, False)]
        final = cross(plus(*ends, piece(1, 0, True)))
        finals = [final]
    else:
        for forward in (True, False):
            crossed[CROSS, forward] = cross(chain(1, forward, CROSS))
        finals = crossed[0]
    ends = [chain(0, f, 0) for f in (True, False)]
    total = sum(v.astype(jnp.float32) for v in ends + finals + [piece(0, 0, True)])
    return (total + dec_bias)[None].astype(jnp.bfloat16)


def solution(mesh):
    size, layers = mesh.shape["feat"], mesh.shape["layer"]
    if layers == 4 and size % 2 == 0 and 4 <= size <= 16:
        def per_device(*arrays):
            return ring_form(size, *arrays)
    else:
        per_device = gathered_form
    return jax.shard_map(
        per_device,
        mesh=mesh,
        in_specs=(
            P("layer", "feat", None),
            P("layer", None, "feat"),
            P("layer", "feat"),
            P("layer", None, "feat", None),
            P("layer", None),
        ),
        out_specs=P("layer", "feat", None),
        check_vma=False,
    )
```

```python
import jax
import jax.numpy as jnp
from jax import lax
from jax.sharding import PartitionSpec as P


def gathered_form(resid_in, enc_weight, enc_bias, dec_weight, dec_bias):
    preact = (
        jnp.dot(
            lax.all_gather(resid_in, "feat", axis=1, tiled=True)[0],
            enc_weight[0],
            preferred_element_type=jnp.float32,
        )
        + enc_bias[0][None, :]
    )
    actives = jnp.maximum(preact, 0.0).astype(jnp.bfloat16)[None]
    source = lax.axis_index("layer")
    total_rows = actives.shape[1]
    model_width = dec_weight.shape[3]
    incoming = lax.all_to_all(dec_weight, "layer", split_axis=1, concat_axis=0, tiled=True)
    every_actives = lax.all_gather(actives, "layer", axis=0, tiled=True)

    def accumulate(earlier, running):
        weight = lax.dynamic_index_in_dim(incoming, earlier, 0, keepdims=False)[0]
        rows = lax.dynamic_index_in_dim(every_actives, earlier, 0, keepdims=False)
        return running + jnp.dot(rows, weight, preferred_element_type=jnp.float32)

    start_sum = jnp.zeros((total_rows, model_width), jnp.float32)
    own_sum = lax.fori_loop(0, source + 1, accumulate, start_sum)
    summed = lax.psum_scatter(own_sum[None], "feat", scatter_dimension=1, tiled=True)
    return (summed + dec_bias[:, None, :]).astype(jnp.bfloat16)


def ring_of(size):
    return list(range(0, size, 2)) + list(range(size - 1, 0, -2))


def ring_form(size, resid_in, enc_weight, enc_bias, dec_weight, dec_bias):
    far = size // 2
    order = ring_of(size)
    ahead = [(order[i], order[(i + 1) % size]) for i in range(size)]
    back = [(b, a) for a, b in ahead]
    swap = [(0, 1), (1, 0), (2, 3), (3, 2)]
    over = [(0, 2), (1, 3)]

    layer = lax.axis_index("layer")
    core = layer % 2
    rows = resid_in[0]
    count = rows.shape[0]
    half = count // 2

    def decoder(weights, target):
        return lax.dynamic_index_in_dim(weights[0], target, 0, keepdims=False)

    give = jnp.stack([jnp.where(core == 0, decoder(dec_weight, jnp.minimum(layer + 1, 3)), 0), decoder(dec_weight, 3 - core)])
    give = lax.optimization_barrier(give)
    take = lax.ppermute(give, "layer", swap)
    near = jnp.concatenate([decoder(dec_weight, layer), take[0]], axis=0)
    upper = jnp.concatenate([decoder(dec_weight, 2 + core), take[1]], axis=0)
    near, upper = lax.optimization_barrier((near, upper))

    fwd = [rows]
    bwd = [rows]
    for _ in range(1, far):
        fwd.append(lax.ppermute(fwd[-1], "feat", ahead))
        bwd.append(lax.ppermute(bwd[-1], "feat", back))
    ends = [lax.ppermute(fwd[-1][:half], "feat", ahead), lax.ppermute(bwd[-1][half:], "feat", back)]
    chunks = [rows] + [jnp.concatenate([bwd[d], fwd[d]], axis=0) for d in range(1, far)] + [jnp.concatenate(ends, axis=0)]

    made = []
    for chunk in chunks:
        preact = jnp.dot(chunk, enc_weight[0], preferred_element_type=jnp.float32) + enc_bias[0][None, :]
        own = jnp.maximum(preact, 0.0).astype(jnp.bfloat16)
        other = lax.ppermute(own, "layer", swap)
        both = jnp.concatenate([own, other], axis=1)
        pair = []
        for w in (near, upper):
            pair.append(jnp.dot(both, w, preferred_element_type=jnp.float32).astype(jnp.bfloat16))
        made.append([lax.optimization_barrier(v) for v in pair])

    def piece(which, distance, forward, part):
        full = made[distance][which]
        if distance == far:
            return lax.optimization_barrier(full[part * half : (part + 1) * half])
        first = (0 if forward else count) + part * half
        return lax.optimization_barrier(full[first : first + half])

    def plus(*values):
        total = values[0].astype(jnp.float32)
        for v in values[1:]:
            total = total + v.astype(jnp.float32)
        return total.astype(jnp.bfloat16)

    ways = [(True, 0), (True, 1), (False, 0), (False, 1)]
    begins = {w: far if w[0] == (w[1] == 0) else far - 1 for w in ways}

    got = lax.ppermute(jnp.concatenate([made[1][1], made[0][1]], axis=0), "layer", over)
    straight = got[2 * count :]
    made[1][0] = lax.optimization_barrier(plus(made[1][0], got[: 2 * count]))

    crossed = {}

    def chain(which, way, stop):
        forward, part = way
        value = piece(which, begins[way], forward, part)
        for distance in range(begins[way] - 1, stop - 1, -1):
            got = lax.ppermute(value, "feat", ahead if forward else back)
            if distance == 0:
                return got
            extra = [crossed[way]] if which == 0 and distance == CROSS else []
            value = plus(got, piece(which, distance, forward, part), *extra)
        return value

    for pair in (((True, 1), (False, 0)), ((True, 0), (False, 1))):
        got = lax.ppermute(jnp.concatenate([chain(1, w, CROSS) for w in pair], axis=0), "layer", over)
        for i, w in enumerate(pair):
            crossed[w] = lax.optimization_barrier(got[i * half : (i + 1) * half])
    joined = [jnp.concatenate([chain(0, (f, part), 0) for part in (0, 1)], axis=0) for f in (True, False)]
    total = sum(v.astype(jnp.float32) for v in joined + [straight, made[0][0]])
    return (total + dec_bias)[None].astype(jnp.bfloat16)


CROSS = 2


def solution(mesh):
    size, layers = mesh.shape["feat"], mesh.shape["layer"]
    if layers == 4 and size % 2 == 0 and 6 <= size <= 16:
        def per_device(*arrays):
            return ring_form(size, *arrays)
    else:
        per_device = gathered_form
    return jax.shard_map(
        per_device,
        mesh=mesh,
        in_specs=(
            P("layer", "feat", None),
            P("layer", None, "feat"),
            P("layer", "feat"),
            P("layer", None, "feat", None),
            P("layer", None),
        ),
        out_specs=P("layer", "feat", None),
        check_vma=False,
    )
```

```python
import jax
import jax.numpy as jnp
from jax import lax
from jax.experimental import pallas as pl
from jax.experimental.pallas import tpu as pltpu
from jax.sharding import PartitionSpec as P


def gathered_form(resid_in, enc_weight, enc_bias, dec_weight, dec_bias):
    preact = (
        jnp.dot(
            lax.all_gather(resid_in, "feat", axis=1, tiled=True)[0],
            enc_weight[0],
            preferred_element_type=jnp.float32,
        )
        + enc_bias[0][None, :]
    )
    actives = jnp.maximum(preact, 0.0).astype(jnp.bfloat16)[None]
    source = lax.axis_index("layer")
    total_rows = actives.shape[1]
    model_width = dec_weight.shape[3]
    incoming = lax.all_to_all(dec_weight, "layer", split_axis=1, concat_axis=0, tiled=True)
    every_actives = lax.all_gather(actives, "layer", axis=0, tiled=True)

    def accumulate(earlier, running):
        weight = lax.dynamic_index_in_dim(incoming, earlier, 0, keepdims=False)[0]
        rows = lax.dynamic_index_in_dim(every_actives, earlier, 0, keepdims=False)
        return running + jnp.dot(rows, weight, preferred_element_type=jnp.float32)

    start_sum = jnp.zeros((total_rows, model_width), jnp.float32)
    own_sum = lax.fori_loop(0, source + 1, accumulate, start_sum)
    summed = lax.psum_scatter(own_sum[None], "feat", scatter_dimension=1, tiled=True)
    return (summed + dec_bias[:, None, :]).astype(jnp.bfloat16)


def spread(bias, count):
    def body(bias_ref, out_ref):
        out_ref[...] = jnp.broadcast_to(bias_ref[...], out_ref.shape)

    return pl.pallas_call(
        body,
        out_shape=jax.ShapeDtypeStruct((count, bias.shape[1]), bias.dtype),
        compiler_params=pltpu.CompilerParams(vmem_limit_bytes=2**21),
    )(bias)


def ring_of(size):
    return list(range(0, size, 2)) + list(range(size - 1, 0, -2))


def ring_form(size, resid_in, enc_weight, enc_bias, dec_weight, dec_bias):
    far = size // 2
    order = ring_of(size)
    ahead = [(order[i], order[(i + 1) % size]) for i in range(size)]
    back = [(b, a) for a, b in ahead]
    swap = [(0, 1), (1, 0), (2, 3), (3, 2)]
    over = [(0, 2), (1, 3)]

    layer = lax.axis_index("layer")
    core = layer % 2
    rows = resid_in[0]
    count = rows.shape[0]
    half = count // 2

    bias_rows = spread(dec_bias, count)

    def decoder(weights, target):
        return lax.dynamic_index_in_dim(weights[0], target, 0, keepdims=False)

    give = jnp.stack([jnp.where(core == 0, decoder(dec_weight, jnp.minimum(layer + 1, 3)), 0), decoder(dec_weight, 3 - core)])
    give = lax.optimization_barrier(give)
    take = lax.ppermute(give, "layer", swap)
    near = jnp.concatenate([decoder(dec_weight, layer), take[0]], axis=0)
    upper = jnp.concatenate([decoder(dec_weight, 2 + core), take[1]], axis=0)
    near, upper = lax.optimization_barrier((near, upper))

    fwd = [rows]
    bwd = [rows]
    for _ in range(1, far):
        fwd.append(lax.ppermute(fwd[-1], "feat", ahead))
        bwd.append(lax.ppermute(bwd[-1], "feat", back))
    ends = [lax.ppermute(fwd[-1][:half], "feat", ahead), lax.ppermute(bwd[-1][half:], "feat", back)]
    chunks = [rows] + [jnp.concatenate([bwd[d], fwd[d]], axis=0) for d in range(1, far)] + [jnp.concatenate(ends, axis=0)]

    made = []
    for chunk in chunks:
        preact = jnp.dot(chunk, enc_weight[0], preferred_element_type=jnp.float32) + enc_bias[0][None, :]
        own = jnp.maximum(preact, 0.0).astype(jnp.bfloat16)
        other = lax.ppermute(own, "layer", swap)
        both = jnp.concatenate([own, other], axis=1)
        pair = []
        for w in (near, upper):
            pair.append(jnp.dot(both, w, preferred_element_type=jnp.float32).astype(jnp.bfloat16))
        made.append([lax.optimization_barrier(v) for v in pair])

    def piece(which, distance, forward, part):
        full = made[distance][which]
        if distance == far:
            return lax.optimization_barrier(full[part * half : (part + 1) * half])
        first = (0 if forward else count) + part * half
        return lax.optimization_barrier(full[first : first + half])

    def plus(*values):
        total = values[0].astype(jnp.float32)
        for v in values[1:]:
            total = total + v.astype(jnp.float32)
        return total.astype(jnp.bfloat16)

    ways = [(True, 0), (True, 1), (False, 0), (False, 1)]
    begins = {w: far if w[0] == (w[1] == 0) else far - 1 for w in ways}

    got = lax.ppermute(jnp.concatenate([made[1][1], made[0][1]], axis=0), "layer", over)
    straight = got[2 * count :]
    made[1][0] = lax.optimization_barrier(plus(made[1][0], got[: 2 * count]))

    crossed = {}

    def chain(which, way, stop):
        forward, part = way
        value = piece(which, begins[way], forward, part)
        for distance in range(begins[way] - 1, stop - 1, -1):
            got = lax.ppermute(value, "feat", ahead if forward else back)
            if distance == 0:
                return got
            extra = [crossed[way]] if which == 0 and distance == CROSS else []
            value = plus(got, piece(which, distance, forward, part), *extra)
        return value

    for pair in (((True, 1), (False, 0)), ((True, 0), (False, 1))):
        got = lax.ppermute(jnp.concatenate([chain(1, w, CROSS) for w in pair], axis=0), "layer", over)
        for i, w in enumerate(pair):
            crossed[w] = lax.optimization_barrier(got[i * half : (i + 1) * half])
    joined = [jnp.concatenate([chain(0, (f, part), 0) for part in (0, 1)], axis=0) for f in (True, False)]
    total = sum(v.astype(jnp.float32) for v in joined + [straight, made[0][0]])
    return (total + bias_rows)[None].astype(jnp.bfloat16)


CROSS = 2


def solution(mesh):
    size, layers = mesh.shape["feat"], mesh.shape["layer"]
    if layers == 4 and size % 2 == 0 and 6 <= size <= 16:
        def per_device(*arrays):
            return ring_form(size, *arrays)
    else:
        per_device = gathered_form
    return jax.shard_map(
        per_device,
        mesh=mesh,
        in_specs=(
            P("layer", "feat", None),
            P("layer", None, "feat"),
            P("layer", "feat"),
            P("layer", None, "feat", None),
            P("layer", None),
        ),
        out_specs=P("layer", "feat", None),
        check_vma=False,
    )
```

```python
import jax
import jax.numpy as jnp
from jax import lax
from jax.experimental import pallas as pl
from jax.experimental.pallas import tpu as pltpu
from jax.sharding import PartitionSpec as P


def gathered_form(resid_in, enc_weight, enc_bias, dec_weight, dec_bias):
    preact = (
        jnp.dot(
            lax.all_gather(resid_in, "feat", axis=1, tiled=True)[0],
            enc_weight[0],
            preferred_element_type=jnp.float32,
        )
        + enc_bias[0][None, :]
    )
    actives = jnp.maximum(preact, 0.0).astype(jnp.bfloat16)[None]
    source = lax.axis_index("layer")
    total_rows = actives.shape[1]
    model_width = dec_weight.shape[3]
    incoming = lax.all_to_all(dec_weight, "layer", split_axis=1, concat_axis=0, tiled=True)
    every_actives = lax.all_gather(actives, "layer", axis=0, tiled=True)

    def accumulate(earlier, running):
        weight = lax.dynamic_index_in_dim(incoming, earlier, 0, keepdims=False)[0]
        rows = lax.dynamic_index_in_dim(every_actives, earlier, 0, keepdims=False)
        return running + jnp.dot(rows, weight, preferred_element_type=jnp.float32)

    start_sum = jnp.zeros((total_rows, model_width), jnp.float32)
    own_sum = lax.fori_loop(0, source + 1, accumulate, start_sum)
    summed = lax.psum_scatter(own_sum[None], "feat", scatter_dimension=1, tiled=True)
    return (summed + dec_bias[:, None, :]).astype(jnp.bfloat16)


def spread(bias, count):
    def body(bias_ref, out_ref):
        out_ref[...] = jnp.broadcast_to(bias_ref[...], out_ref.shape)

    return pl.pallas_call(
        body,
        out_shape=jax.ShapeDtypeStruct((count, bias.shape[1]), bias.dtype),
        compiler_params=pltpu.CompilerParams(vmem_limit_bytes=2**21),
    )(bias)


def ring_of(size):
    return list(range(0, size, 2)) + list(range(size - 1, 0, -2))


def ring_form(size, resid_in, enc_weight, enc_bias, dec_weight, dec_bias):
    far = size // 2
    order = ring_of(size)
    ahead = [(order[i], order[(i + 1) % size]) for i in range(size)]
    back = [(b, a) for a, b in ahead]
    swap = [(0, 1), (1, 0), (2, 3), (3, 2)]
    over = [(0, 2), (1, 3)]

    layer = lax.axis_index("layer")
    core = layer % 2
    rows = resid_in[0]
    count = rows.shape[0]
    half = count // 2

    bias_rows = spread(dec_bias, count)

    def decoder(weights, target):
        return lax.dynamic_index_in_dim(weights[0], target, 0, keepdims=False)

    give = jnp.stack([jnp.where(core == 0, decoder(dec_weight, jnp.minimum(layer + 1, 3)), 0), decoder(dec_weight, 3 - core)])
    give = lax.optimization_barrier(give)
    take = lax.ppermute(give, "layer", swap)
    near = jnp.concatenate([decoder(dec_weight, layer), take[0]], axis=0)
    upper = jnp.concatenate([decoder(dec_weight, 2 + core), take[1]], axis=0)
    near, upper = lax.optimization_barrier((near, upper))

    fwd = [(rows,), (lax.ppermute(rows, "feat", ahead),)]
    bwd = [(rows,), (lax.ppermute(rows, "feat", back),)]
    for _ in range(2, far):
        for line, pairs in ((fwd, ahead), (bwd, back)):
            parts = line[-1] if len(line[-1]) > 1 else (line[-1][0][:half], line[-1][0][half:])
            line.append(tuple(lax.ppermute(parts[i], "feat", pairs) for i in (0, 1)))
    ends = [lax.ppermute(fwd[-1][0], "feat", ahead), lax.ppermute(bwd[-1][1], "feat", back)]
    chunks = [rows] + [jnp.concatenate(bwd[d] + fwd[d], axis=0) for d in range(1, far)] + [jnp.concatenate(ends, axis=0)]

    made = []
    for chunk in chunks:
        preact = jnp.dot(chunk, enc_weight[0], preferred_element_type=jnp.float32) + enc_bias[0][None, :]
        own = jnp.maximum(preact, 0.0).astype(jnp.bfloat16)
        other = lax.ppermute(own, "layer", swap)
        both = jnp.concatenate([own, other], axis=1)
        pair = []
        for w in (near, upper):
            pair.append(jnp.dot(both, w, preferred_element_type=jnp.float32).astype(jnp.bfloat16))
        made.append([lax.optimization_barrier(v) for v in pair])

    def piece(which, distance, forward, part):
        full = made[distance][which]
        if distance == far:
            return lax.optimization_barrier(full[part * half : (part + 1) * half])
        first = (0 if forward else count) + part * half
        return lax.optimization_barrier(full[first : first + half])

    def plus(*values):
        total = values[0].astype(jnp.float32)
        for v in values[1:]:
            total = total + v.astype(jnp.float32)
        return total.astype(jnp.bfloat16)

    ways = [(True, 0), (True, 1), (False, 0), (False, 1)]
    begins = {w: far if w[0] == (w[1] == 0) else far - 1 for w in ways}

    got = lax.ppermute(made[1][1], "layer", over)
    straight = lax.ppermute(made[0][1], "layer", over)
    made[1][0] = lax.optimization_barrier(plus(made[1][0], got))

    crossed = {}

    def chain(which, way, stop):
        forward, part = way
        value = piece(which, begins[way], forward, part)
        for distance in range(begins[way] - 1, stop - 1, -1):
            got = lax.ppermute(value, "feat", ahead if forward else back)
            if distance == 0:
                return got
            extra = [crossed[way]] if which == 0 and distance == CROSS else []
            value = plus(got, piece(which, distance, forward, part), *extra)
        return value

    for pair in (((True, 1), (False, 0)), ((True, 0), (False, 1))):
        got = lax.ppermute(jnp.concatenate([chain(1, w, CROSS) for w in pair], axis=0), "layer", over)
        for i, w in enumerate(pair):
            crossed[w] = lax.optimization_barrier(got[i * half : (i + 1) * half])
    joined = [jnp.concatenate([chain(0, (f, part), 0) for part in (0, 1)], axis=0) for f in (True, False)]
    total = sum(v.astype(jnp.float32) for v in joined + [straight, made[0][0]])
    return (total + bias_rows)[None].astype(jnp.bfloat16)


CROSS = 2


def solution(mesh):
    size, layers = mesh.shape["feat"], mesh.shape["layer"]
    if layers == 4 and size % 2 == 0 and 6 <= size <= 16:
        def per_device(*arrays):
            return ring_form(size, *arrays)
    else:
        per_device = gathered_form
    return jax.shard_map(
        per_device,
        mesh=mesh,
        in_specs=(
            P("layer", "feat", None),
            P("layer", None, "feat"),
            P("layer", "feat"),
            P("layer", None, "feat", None),
            P("layer", None),
        ),
        out_specs=P("layer", "feat", None),
        check_vma=False,
    )
```

```python
import jax
import jax.numpy as jnp
from jax import lax
from jax.experimental import pallas as pl
from jax.experimental.pallas import tpu as pltpu
from jax.sharding import PartitionSpec as P


def gathered_form(resid_in, enc_weight, enc_bias, dec_weight, dec_bias):
    preact = (
        jnp.dot(
            lax.all_gather(resid_in, "feat", axis=1, tiled=True)[0],
            enc_weight[0],
            preferred_element_type=jnp.float32,
        )
        + enc_bias[0][None, :]
    )
    actives = jnp.maximum(preact, 0.0).astype(jnp.bfloat16)[None]
    source = lax.axis_index("layer")
    total_rows = actives.shape[1]
    model_width = dec_weight.shape[3]
    incoming = lax.all_to_all(dec_weight, "layer", split_axis=1, concat_axis=0, tiled=True)
    every_actives = lax.all_gather(actives, "layer", axis=0, tiled=True)

    def accumulate(earlier, running):
        weight = lax.dynamic_index_in_dim(incoming, earlier, 0, keepdims=False)[0]
        rows = lax.dynamic_index_in_dim(every_actives, earlier, 0, keepdims=False)
        return running + jnp.dot(rows, weight, preferred_element_type=jnp.float32)

    start_sum = jnp.zeros((total_rows, model_width), jnp.float32)
    own_sum = lax.fori_loop(0, source + 1, accumulate, start_sum)
    summed = lax.psum_scatter(own_sum[None], "feat", scatter_dimension=1, tiled=True)
    return (summed + dec_bias[:, None, :]).astype(jnp.bfloat16)


def spread(bias, count):
    def body(bias_ref, out_ref):
        out_ref[...] = jnp.broadcast_to(bias_ref[...], out_ref.shape)

    return pl.pallas_call(
        body,
        out_shape=jax.ShapeDtypeStruct((count, bias.shape[1]), bias.dtype),
        compiler_params=pltpu.CompilerParams(vmem_limit_bytes=2**21),
    )(bias)


def ring_of(size):
    return list(range(0, size, 2)) + list(range(size - 1, 0, -2))


def ring_form(size, resid_in, enc_weight, enc_bias, dec_weight, dec_bias):
    far = size // 2
    order = ring_of(size)
    ahead = [(order[i], order[(i + 1) % size]) for i in range(size)]
    back = [(b, a) for a, b in ahead]
    swap = [(0, 1), (1, 0), (2, 3), (3, 2)]
    over = [(0, 2), (1, 3)]

    layer = lax.axis_index("layer")
    core = layer % 2
    rows = resid_in[0]
    count = rows.shape[0]
    half = count // 2

    bias_rows = spread(dec_bias, count)

    def decoder(weights, target):
        return lax.dynamic_index_in_dim(weights[0], target, 0, keepdims=False)

    give = jnp.stack([jnp.where(core == 0, decoder(dec_weight, jnp.minimum(layer + 1, 3)), 0), decoder(dec_weight, 3 - core)])
    give = lax.optimization_barrier(give)
    take = lax.ppermute(give, "layer", swap)
    near = jnp.concatenate([decoder(dec_weight, layer), take[0]], axis=0)
    upper = jnp.concatenate([decoder(dec_weight, 2 + core), take[1]], axis=0)
    near, upper = lax.optimization_barrier((near, upper))

    fwd = [(rows,), (lax.ppermute(rows, "feat", ahead),)]
    bwd = [(rows,), (lax.ppermute(rows, "feat", back),)]
    for _ in range(2, far):
        for line, pairs in ((fwd, ahead), (bwd, back)):
            parts = line[-1] if len(line[-1]) > 1 else (line[-1][0][:half], line[-1][0][half:])
            line.append(tuple(lax.ppermute(parts[i], "feat", pairs) for i in (0, 1)))
    ends = [lax.ppermute(fwd[-1][0], "feat", ahead), lax.ppermute(bwd[-1][1], "feat", back)]
    chunks = [rows] + [jnp.concatenate(bwd[d] + fwd[d], axis=0) for d in range(1, far)] + [jnp.concatenate(ends, axis=0)]

    made = []
    for d, chunk in enumerate(chunks):
        preact = jnp.dot(chunk, enc_weight[0], preferred_element_type=jnp.float32) + enc_bias[0][None, :]
        own = jnp.maximum(preact, 0.0).astype(jnp.bfloat16)
        other = lax.ppermute(own, "layer", swap)
        both = jnp.concatenate([own, other], axis=1)
        pair = []
        for name, w in (("near", near), ("upper", upper)):
            total = jnp.dot(both, w, preferred_element_type=jnp.float32)
            pair.append(total if name == "near" and d < far - 1 else total.astype(jnp.bfloat16))
        made.append([lax.optimization_barrier(v) for v in pair])

    def piece(which, distance, forward, part):
        full = made[distance][which]
        if distance == far:
            return lax.optimization_barrier(full[part * half : (part + 1) * half])
        first = (0 if forward else count) + part * half
        return lax.optimization_barrier(full[first : first + half])

    def plus(*values):
        total = values[0].astype(jnp.float32)
        for v in values[1:]:
            total = total + v.astype(jnp.float32)
        return total.astype(jnp.bfloat16)

    ways = [(True, 0), (True, 1), (False, 0), (False, 1)]
    begins = {w: far if w[0] == (w[1] == 0) else far - 1 for w in ways}

    got = lax.ppermute(made[1][1], "layer", over)
    straight = lax.ppermute(made[0][1], "layer", over)
    made[1][0] = lax.optimization_barrier(made[1][0] + got.astype(jnp.float32))

    crossed = {}

    def chain(which, way, stop):
        forward, part = way
        value = piece(which, begins[way], forward, part)
        for distance in range(begins[way] - 1, stop - 1, -1):
            got = lax.ppermute(value, "feat", ahead if forward else back)
            if distance == 0:
                return got
            extra = [crossed[way]] if which == 0 and distance == CROSS else []
            value = plus(got, piece(which, distance, forward, part), *extra)
        return value

    for pair in (((True, 1), (False, 0)), ((True, 0), (False, 1))):
        got = lax.ppermute(jnp.concatenate([chain(1, w, CROSS) for w in pair], axis=0), "layer", over)
        for i, w in enumerate(pair):
            crossed[w] = lax.optimization_barrier(got[i * half : (i + 1) * half])
    joined = [jnp.concatenate([chain(0, (f, part), 0) for part in (0, 1)], axis=0) for f in (True, False)]
    total = sum(v.astype(jnp.float32) for v in joined + [straight, made[0][0]])
    return (total + bias_rows)[None].astype(jnp.bfloat16)


CROSS = 2


def solution(mesh):
    size, layers = mesh.shape["feat"], mesh.shape["layer"]
    if layers == 4 and size % 2 == 0 and 6 <= size <= 16:
        def per_device(*arrays):
            return ring_form(size, *arrays)
    else:
        per_device = gathered_form
    return jax.shard_map(
        per_device,
        mesh=mesh,
        in_specs=(
            P("layer", "feat", None),
            P("layer", None, "feat"),
            P("layer", "feat"),
            P("layer", None, "feat", None),
            P("layer", None),
        ),
        out_specs=P("layer", "feat", None),
        check_vma=False,
    )
```
